256 devices in a mesh: dp: 16 (over y_hi, z), ctx: 16 (over y_lo, x, core).
Axes of the slice: x: 4, y: 4 (y_hi: 2, y_lo: 2; y = y_hi * 2 + y_lo), z: 8, core: 2. Of those that a mesh axis runs over, the one named last changes fastest.
Arguments:
- embeds: bfloat16 [16, 2048, 4096], P('dp', 'ctx'), may hold values from -6 to 6
- norm_gain: float32 [4096], replicated, may hold values from 0.1 to 1.9
- w_key: bfloat16 [4096, 512], P('dp'), may hold values from -0.09375 to 0.09375
- w_value: bfloat16 [4096, 512], P('dp'), may hold values from -0.09375 to 0.09375
- queries: bfloat16 [16, 2048, 4096], P('dp', 'ctx'), may hold values from -85 to 85
- d_out: bfloat16 [16, 2048, 4096], P('dp', 'ctx'), may hold values from -6 to 6
- block_doc: int32 [16, 16], P('dp'), may hold values from 0 to 3, never falling along the last dimension, each value on 1 to 8 neighbouring positions
- slot_order: int32 [16, 32], P('dp'), may hold values from 0 to 31, each once within a row
Outputs:
- grad_embed: bfloat16 [16, 2048, 4096], P('dp', 'ctx')
The draws below stay inside these ranges and needn't reach their ends.
Inputs may be any that keep to these rules, and one draw needn't show every extreme that they name: `block_doc`: along the blocks of a sequence the document number never falls; each of the 4 documents covers 1 to 8 blocks, and one covers exactly 8. `slot_order`: each row holds every number from 0 to 31 once.
All inputs are finite; a program needn't handle non-finite values.
Results may differ from the reference program's by a relative error of at most 0.035.
The reference program's roundings to bfloat16 on the way count: a program that leaves them out, or rounds other values in their place, can miss the bound.
Values may be sent and summed in bfloat16 or wider, within the bound.
No kernel may reach another device: no remote copies, remote signals or barrier semaphores. Data moves between devices by JAX's collectives and lax.ppermute only.
A program may use at most 192 MiB of HBM per device.

```python
import math
import jax
import jax.numpy as jnp
import numpy as np
from jax import lax

D = 4096
HEADS = 32
KV_HEADS = 4
HEAD = 128
GROUP = 8
DOC_BLOCK = 128
BATCH = 16
SEQ = 2048
HALF_TOK = 64
SLOTS = 32
NBLK = 16
NDOCS = 4
MOST_BLK = 8


def draw_queries(key, part):
    dims = (BATCH, SEQ, HEADS * HEAD)
    normal_part = jax.random.normal(key, dims, jnp.float32)
    return jnp.clip(normal_part, -6.0, 6.0).astype(jnp.bfloat16)


def block_levels(own_key, shape, shards, least, top_value):
    gain, own = 1.0, jax.random.fold_in(own_key, 6)
    for dim, blocks in shards:
        heights = jnp.exp(jax.random.uniform(jax.random.fold_in(own, dim), (blocks,), jnp.float32, least / len(shards), top_value / len(shards)))
        gain = gain * jnp.repeat(heights, shape[dim] // blocks).reshape([-1 if axis == dim else 1 for axis in range(len(shape))])
    return gain


def length_profile(count, total, bound, slope):
    portions = [(1 << 20) // math.isqrt(rank ** slope) + 1 for rank in range(2, count + 1)]
    spare, holding = total - bound - (count - 1), [1] * (count - 1)
    while spare > 0:
        candidates = [i for i in range(count - 1) if holding[i] < bound]
        mass, left = sum([portions[i] for i in candidates]), spare
        for i in candidates:
            addition = min(bound - holding[i], max(1, left * portions[i] // mass), spare)
            holding[i] = holding[i] + addition
            spare = spare - addition
    return np.array([bound] + holding)


def ragged_sizes(own_key, number_of, total, bound, lean):
    if number_of == 2:
        one = jax.random.randint(own_key, (), max(1, total - bound), min(bound, total - 1) + 1)
        return jnp.stack([one, total - one])
    lengths = jnp.asarray(length_profile(number_of, total, bound, lean), jnp.int32)
    couples = (number_of - 1) // 2
    giver, receiver = lengths[1:1 + 2 * couples:2], lengths[2:2 + 2 * couples:2]
    slack = jnp.minimum(giver - 1, bound - receiver)
    moved = jax.random.randint(jax.random.fold_in(own_key, 1), (couples,), 0, 1 << 20) % (slack + 1)
    lengths = lengths.at[1:1 + 2 * couples:2].set(giver - moved).at[2:2 + 2 * couples:2].set(receiver + moved)
    return lengths[jax.random.permutation(jax.random.fold_in(own_key, 2), number_of)]


def normal_values(key, shape, scale, reach, cuts=(), kind=jnp.bfloat16):
    array = scale * jax.random.normal(key, shape, jnp.float32)
    if cuts:
        array = array * block_levels(key, shape, cuts, -0.22, 0.18)
    return jnp.clip(array, -reach, reach).astype(kind)


def setup_inputs(seed: int = 0) -> dict:
    splits = jax.random.split(jax.random.key(seed), 9)
    embeds = normal_values(splits[0], (BATCH, SEQ, D), 1.0, 6.0, ((0, 16), (1, 16)))
    norm_gain = jnp.clip(1.0 + 0.18 * jax.random.normal(splits[1], (D,), jnp.float32), 0.1, 1.9)
    w_key = normal_values(splits[2], (D, KV_HEADS * HEAD), D ** -0.5, 0.09375, ((0, 16),))
    w_value = normal_values(splits[3], (D, KV_HEADS * HEAD), D ** -0.5, 0.09375, ((0, 16),))
    queries = draw_queries(jax.random.fold_in(splits[8], 71), 0)
    d_out = normal_values(splits[5], (BATCH, SEQ, HEADS * HEAD), 1.0, 6.0, ((0, 16), (1, 16)))
    block_doc = jax.vmap(lambda own: jnp.searchsorted(jnp.cumsum(ragged_sizes(own, NDOCS, NBLK, MOST_BLK, 1)), jnp.arange(NBLK), side="right"))(jax.random.split(splits[6], BATCH)).reshape((BATCH, NBLK)).astype(jnp.int32)
    slot_order = jax.vmap(lambda own: jax.random.permutation(own, SLOTS))(jax.random.split(splits[7], BATCH)).reshape((BATCH, SLOTS)).astype(jnp.int32)
    return dict(embeds=embeds, norm_gain=norm_gain, w_key=w_key, w_value=w_value, queries=queries, d_out=d_out, block_doc=block_doc, slot_order=slot_order)


def reference(embeds, norm_gain, w_key, w_value, queries, d_out, block_doc, slot_order):
    joined = jnp.concatenate([w_key, w_value], axis=1)
    kv_width = KV_HEADS * HEAD
    score_scale = HEAD ** (-0.5)

    def one_sequence(inputs):
        embed_rows, query_rows, dout_rows, doc_table, order_row = inputs
        row_ids = jnp.arange(SEQ, dtype=jnp.int32)
        position = (order_row[row_ids // HALF_TOK] * HALF_TOK + row_ids % HALF_TOK).astype(jnp.int32)
        document = doc_table[position // DOC_BLOCK]
        allowed = (position[None, :] <= position[:, None]) & (document[None, :] == document[:, None])
        as_float = embed_rows.astype(jnp.float32)
        inv_rms = lax.rsqrt(lax.optimization_barrier(jnp.mean(as_float * as_float, axis=-1, keepdims=True)) + 1e-05)
        normed = (as_float * inv_rms * norm_gain).astype(jnp.bfloat16)
        projected = jnp.dot(normed, joined, preferred_element_type=jnp.float32).astype(jnp.bfloat16)
        projected = lax.optimization_barrier(projected)
        key_grads = []
        value_grads = []
        for kv_head in range(KV_HEADS):
            first_col = kv_head * GROUP * HEAD
            last_col = (kv_head + 1) * GROUP * HEAD
            query_group = query_rows[:, first_col:last_col].reshape(SEQ, GROUP, HEAD).astype(jnp.float32)
            dout_group = dout_rows[:, first_col:last_col].reshape(SEQ, GROUP, HEAD).astype(jnp.float32)
            key_group = projected[:, kv_head * HEAD:(kv_head + 1) * HEAD].astype(jnp.float32)
            value_group = projected[:, kv_width + kv_head * HEAD:kv_width + (kv_head + 1) * HEAD].astype(jnp.float32)
            scores = jnp.einsum('thd,kd->htk', query_group, key_group) * score_scale
            row_max = lax.optimization_barrier(jnp.max(jnp.where(allowed[None], scores, -jnp.inf), axis=-1, keepdims=True))
            raised = jnp.where(allowed[None], jnp.exp(scores - row_max), 0.0)
            soft_probs = raised / lax.optimization_barrier(jnp.sum(raised, axis=-1, keepdims=True))
            probs_half = lax.optimization_barrier(soft_probs.astype(jnp.bfloat16)).astype(jnp.float32)
            attn_out = jnp.einsum('htk,kd->htd', probs_half, value_group)
            row_delta = jnp.einsum('htd,thd->ht', attn_out, dout_group)
            dprobs = jnp.einsum('thd,kd->htk', dout_group, value_group)
            score_grad = (soft_probs * (dprobs - row_delta[..., None]) * score_scale).astype(jnp.bfloat16)
            score_grad = lax.optimization_barrier(score_grad).astype(jnp.float32)
            key_grads.append(jnp.einsum('htk,thd->kd', score_grad, query_group))
            value_grads.append(jnp.einsum('htk,thd->kd', probs_half, dout_group))
        grad_half = jnp.concatenate(key_grads + value_grads, axis=1).astype(jnp.bfloat16)
        grad_normed = jnp.dot(grad_half, joined.T, preferred_element_type=jnp.float32)
        mean_term = lax.optimization_barrier(jnp.mean(as_float * norm_gain * grad_normed, axis=-1, keepdims=True))
        grad_embed = inv_rms * norm_gain * grad_normed - as_float * inv_rms * inv_rms * inv_rms * mean_term
        return grad_embed.astype(jnp.bfloat16)
    return lax.map(one_sequence, (embeds, queries, d_out, block_doc, slot_order))
```

```python
import jax
import jax.numpy as jnp
from jax import lax
from jax.sharding import PartitionSpec as P

HEADS = 32
KV_HEADS = 4
HEAD = 128
DOC_BLOCK = 128


def attend(query_group, dout_group, key_group, value_group, allowed, block_width, score_scale):
    tok_rows, group_size, head_size = query_group.shape
    seq_len = key_group.shape[0]
    block_count = seq_len // block_width
    mask_blocks = allowed.reshape(tok_rows, block_count, block_width)
    live_blocks = jnp.any(mask_blocks, axis=(0, 2))
    mask_blocks = mask_blocks.transpose(1, 0, 2)
    key_blocks = key_group.reshape(block_count, block_width, head_size)
    value_blocks = value_group.reshape(block_count, block_width, head_size)

    def score_block(block_item):
        is_live, key_block, mask_block = block_item
        raw_scores = jnp.einsum(
            "thd,kd->htk", query_group, key_block, preferred_element_type=jnp.float32
        )
        return jnp.where(mask_block[None], raw_scores * score_scale, -jnp.inf)

    scores = lax.map(score_block, (live_blocks, key_blocks, mask_blocks))
    row_max = jnp.max(scores, axis=(0, 3))
    raised = jnp.exp(scores - row_max[None, :, :, None])
    soft_probs = raised / jnp.sum(raised, axis=(0, 3))[None, :, :, None]
    probs_half = soft_probs.astype(jnp.bfloat16)

    def output_block(block_item):
        is_live, prob_half, value_block = block_item
        return jnp.einsum("htk,kd->htd", prob_half, value_block, preferred_element_type=jnp.float32)

    attn_out = jnp.sum(lax.map(output_block, (live_blocks, probs_half, value_blocks)), axis=0)
    row_delta = jnp.einsum("htd,thd->ht", attn_out, dout_group.astype(jnp.float32))

    def grad_block(block_item):
        is_live, prob_block, prob_half, key_block, value_block = block_item
        dprobs = jnp.einsum(
            "thd,kd->htk", dout_group, value_block, preferred_element_type=jnp.float32
        )
        score_grad = (prob_block * (dprobs - row_delta[..., None]) * score_scale).astype(
            jnp.bfloat16
        )
        key_grad = jnp.einsum(
            "htk,thd->kd", score_grad, query_group, preferred_element_type=jnp.float32
        )
        value_grad = jnp.einsum(
            "htk,thd->kd", prob_half, dout_group, preferred_element_type=jnp.float32
        )
        return (key_grad, value_grad)

    key_grad, value_grad = lax.map(
        grad_block, (live_blocks, soft_probs, probs_half, key_blocks, value_blocks)
    )
    return (key_grad.reshape(seq_len, head_size), value_grad.reshape(seq_len, head_size))


def gather_weights(local_w, ctx_ways):
    shard_rows = local_w.shape[0]
    piece_rows = shard_rows // ctx_ways
    start = lax.axis_index("ctx") * piece_rows
    piece = lax.dynamic_slice_in_dim(local_w, start, piece_rows, axis=0)
    by_shard = lax.all_gather(piece, "dp", axis=0, tiled=False)
    full = lax.all_gather(by_shard, "ctx", axis=1, tiled=False)
    return full.reshape(-1, local_w.shape[1])


def body(embeds, norm_gain, w_key, w_value, queries, d_out, block_doc, slot_order):
    embed_rows = embeds[0]
    tok_rows = embed_rows.shape[0]
    ctx_ways = lax.axis_size("ctx")
    seq_len = tok_rows * ctx_ways
    half_len = tok_rows // 2
    kv_width = KV_HEADS * HEAD
    group_size = HEADS // KV_HEADS
    score_scale = HEAD ** (-0.5)
    as_float = embed_rows.astype(jnp.float32)
    inv_rms = lax.rsqrt(jnp.mean(as_float * as_float, axis=-1, keepdims=True) + 1e-05)
    normed = (as_float * inv_rms * norm_gain).astype(jnp.bfloat16)
    pieces = gather_weights(jnp.concatenate([w_key, w_value], axis=1), ctx_ways)
    pieces = (pieces[:, :kv_width], pieces[:, kv_width:])
    key_proj = jnp.dot(normed, pieces[0], preferred_element_type=jnp.float32)
    value_proj = jnp.dot(normed, pieces[1], preferred_element_type=jnp.float32)
    key_proj = key_proj.astype(jnp.bfloat16)
    value_proj = value_proj.astype(jnp.bfloat16)
    row_ids = jnp.arange(seq_len, dtype=jnp.int32)
    slot_hit = (row_ids // half_len)[:, None] == jnp.arange(2 * ctx_ways, dtype=jnp.int32)[None, :]
    key_pos = (
        jnp.sum(jnp.where(slot_hit, slot_order[0][None, :], 0), axis=1) * half_len
        + row_ids % half_len
    )
    block_hit = (key_pos // DOC_BLOCK)[:, None] == jnp.arange(block_doc.shape[1], dtype=jnp.int32)[
        None, :
    ]
    key_doc = jnp.sum(jnp.where(block_hit, block_doc[0][None, :], 0), axis=1)
    row_start = lax.axis_index("ctx") * tok_rows
    query_pos = lax.dynamic_slice_in_dim(key_pos, row_start, tok_rows)
    query_doc = lax.dynamic_slice_in_dim(key_doc, row_start, tok_rows)
    allowed = (key_pos[None, :] <= query_pos[:, None]) & (key_doc[None, :] == query_doc[:, None])
    key_grads = []
    value_grads = []
    for kv_head in range(KV_HEADS):
        first_col = kv_head * group_size * HEAD
        last_col = (kv_head + 1) * group_size * HEAD
        query_group = queries[0][:, first_col:last_col].reshape(tok_rows, group_size, HEAD)
        dout_group = d_out[0][:, first_col:last_col].reshape(tok_rows, group_size, HEAD)
        head_kv = jnp.concatenate(
            [key_proj[:, kv_head * HEAD : (kv_head + 1) * HEAD],
             value_proj[:, kv_head * HEAD : (kv_head + 1) * HEAD]], axis=1)
        head_kv = lax.all_gather(head_kv, "ctx", axis=0, tiled=True)
        key_group = head_kv[:, :HEAD]
        value_group = head_kv[:, HEAD:]
        key_grad, value_grad = attend(
            query_group, dout_group, key_group, value_group, allowed, seq_len, score_scale
        )
        head_sum = lax.psum_scatter(
            jnp.concatenate([key_grad, value_grad], axis=1).astype(jnp.bfloat16),
            "ctx", scatter_dimension=0, tiled=True)
        key_grads.append(head_sum[:, :HEAD])
        value_grads.append(head_sum[:, HEAD:])
    key_half = jnp.concatenate(key_grads, axis=1)
    value_half = jnp.concatenate(value_grads, axis=1)
    contract = (((1,), (1,)), ((), ()))
    grad_normed = lax.dot_general(
        key_half, pieces[0], contract, preferred_element_type=jnp.float32
    ) + lax.dot_general(value_half, pieces[1], contract, preferred_element_type=jnp.float32)
    mean_term = jnp.mean(as_float * norm_gain * grad_normed, axis=-1, keepdims=True)
    grad_embed = (
        inv_rms * norm_gain * grad_normed - as_float * inv_rms * inv_rms * inv_rms * mean_term
    )
    return grad_embed.astype(jnp.bfloat16)[None]


def solution(mesh):
    in_specs = (
        P("dp", "ctx", None),
        P(),
        P("dp", None),
        P("dp", None),
        P("dp", "ctx", None),
        P("dp", "ctx", None),
        P("dp", None),
        P("dp", None),
    )
    out_specs = P("dp", "ctx", None)
    return jax.shard_map(body, mesh=mesh, in_specs=in_specs, out_specs=out_specs, check_vma=False)
```

```python
import jax
import jax.numpy as jnp
from jax import lax
from jax.sharding import PartitionSpec as P

HEADS = 32
KV_HEADS = 4
HEAD = 128
DOC_BLOCK = 128


def attend(query_group, dout_group, key_group, value_group, allowed, block_width, score_scale):
    tok_rows, group_size, head_size = query_group.shape
    seq_len = key_group.shape[0]
    block_count = seq_len // block_width
    mask_blocks = allowed.reshape(tok_rows, block_count, block_width)
    live_blocks = jnp.any(mask_blocks, axis=(0, 2))
    mask_blocks = mask_blocks.transpose(1, 0, 2)
    key_blocks = key_group.reshape(block_count, block_width, head_size)
    value_blocks = value_group.reshape(block_count, block_width, head_size)

    def score_block(block_item):
        is_live, key_block, mask_block = block_item
        raw_scores = jnp.einsum(
            "thd,kd->htk", query_group, key_block, preferred_element_type=jnp.float32
        )
        return jnp.where(mask_block[None], raw_scores * score_scale, -jnp.inf)

    scores = lax.map(score_block, (live_blocks, key_blocks, mask_blocks))
    row_max = jnp.max(scores, axis=(0, 3))
    raised = jnp.exp(scores - row_max[None, :, :, None])
    soft_probs = raised / jnp.sum(raised, axis=(0, 3))[None, :, :, None]
    probs_half = soft_probs.astype(jnp.bfloat16)

    def output_block(block_item):
        is_live, prob_half, value_block = block_item
        return jnp.einsum("htk,kd->htd", prob_half, value_block, preferred_element_type=jnp.float32)

    attn_out = jnp.sum(lax.map(output_block, (live_blocks, probs_half, value_blocks)), axis=0)
    row_delta = jnp.einsum("htd,thd->ht", attn_out, dout_group.astype(jnp.float32))

    def grad_block(block_item):
        is_live, prob_block, prob_half, key_block, value_block = block_item
        dprobs = jnp.einsum(
            "thd,kd->htk", dout_group, value_block, preferred_element_type=jnp.float32
        )
        score_grad = (prob_block * (dprobs - row_delta[..., None]) * score_scale).astype(
            jnp.bfloat16
        )
        key_grad = jnp.einsum(
            "htk,thd->kd", score_grad, query_group, preferred_element_type=jnp.float32
        )
        value_grad = jnp.einsum(
            "htk,thd->kd", prob_half, dout_group, preferred_element_type=jnp.float32
        )
        return (key_grad, value_grad)

    key_grad, value_grad = lax.map(
        grad_block, (live_blocks, soft_probs, probs_half, key_blocks, value_blocks)
    )
    return (key_grad.reshape(seq_len, head_size), value_grad.reshape(seq_len, head_size))


def gather_weights(local_w, ctx_ways):
    shard_rows = local_w.shape[0]
    piece_rows = shard_rows // ctx_ways
    start = lax.axis_index("ctx") * piece_rows
    piece = lax.dynamic_slice_in_dim(local_w, start, piece_rows, axis=0)
    by_shard = lax.all_gather(piece, "dp", axis=0, tiled=False)
    full = lax.all_gather(by_shard, "ctx", axis=1, tiled=False)
    return full.reshape(-1, local_w.shape[1])


def body(embeds, norm_gain, w_key, w_value, queries, d_out, block_doc, slot_order):
    embed_rows = embeds[0]
    tok_rows = embed_rows.shape[0]
    ctx_ways = lax.axis_size("ctx")
    seq_len = tok_rows * ctx_ways
    half_len = tok_rows // 2
    kv_width = KV_HEADS * HEAD
    group_size = HEADS // KV_HEADS
    score_scale = HEAD ** (-0.5)
    as_float = embed_rows.astype(jnp.float32)
    inv_rms = lax.rsqrt(jnp.mean(as_float * as_float, axis=-1, keepdims=True) + 1e-05)
    normed = (as_float * inv_rms * norm_gain).astype(jnp.bfloat16)
    pieces = gather_weights(jnp.concatenate([w_key, w_value], axis=1), ctx_ways)
    pieces = (pieces[:, :kv_width], pieces[:, kv_width:])
    key_proj = jnp.dot(normed, pieces[0], preferred_element_type=jnp.float32)
    value_proj = jnp.dot(normed, pieces[1], preferred_element_type=jnp.float32)
    local_kv = jnp.concatenate([key_proj, value_proj], axis=1).astype(jnp.bfloat16)
    all_kv = lax.all_gather(local_kv, "ctx", axis=0, tiled=True)
    row_ids = jnp.arange(seq_len, dtype=jnp.int32)
    slot_hit = (row_ids // half_len)[:, None] == jnp.arange(2 * ctx_ways, dtype=jnp.int32)[None, :]
    key_pos = (
        jnp.sum(jnp.where(slot_hit, slot_order[0][None, :], 0), axis=1) * half_len
        + row_ids % half_len
    )
    block_hit = (key_pos // DOC_BLOCK)[:, None] == jnp.arange(block_doc.shape[1], dtype=jnp.int32)[
        None, :
    ]
    key_doc = jnp.sum(jnp.where(block_hit, block_doc[0][None, :], 0), axis=1)
    row_start = lax.axis_index("ctx") * tok_rows
    query_pos = lax.dynamic_slice_in_dim(key_pos, row_start, tok_rows)
    query_doc = lax.dynamic_slice_in_dim(key_doc, row_start, tok_rows)
    allowed = (key_pos[None, :] <= query_pos[:, None]) & (key_doc[None, :] == query_doc[:, None])
    key_grads = []
    value_grads = []
    for kv_head in range(KV_HEADS):
        first_col = kv_head * group_size * HEAD
        last_col = (kv_head + 1) * group_size * HEAD
        query_group = queries[0][:, first_col:last_col].reshape(tok_rows, group_size, HEAD)
        dout_group = d_out[0][:, first_col:last_col].reshape(tok_rows, group_size, HEAD)
        key_group = all_kv[:, kv_head * HEAD : (kv_head + 1) * HEAD]
        value_group = all_kv[:, kv_width + kv_head * HEAD : kv_width + (kv_head + 1) * HEAD]
        key_grad, value_grad = attend(
            query_group, dout_group, key_group, value_group, allowed, seq_len, score_scale
        )
        key_grads.append(key_grad)
        value_grads.append(value_grad)
    grad_terms = jnp.concatenate(key_grads + value_grads, axis=1)
    own_sum = lax.psum_scatter(
        grad_terms.astype(jnp.bfloat16), "ctx", scatter_dimension=0, tiled=True
    )
    key_half = own_sum[:, :kv_width]
    value_half = own_sum[:, kv_width:]
    contract = (((1,), (1,)), ((), ()))
    grad_normed = lax.dot_general(
        key_half, pieces[0], contract, preferred_element_type=jnp.float32
    ) + lax.dot_general(value_half, pieces[1], contract, preferred_element_type=jnp.float32)
    mean_term = jnp.mean(as_float * norm_gain * grad_normed, axis=-1, keepdims=True)
    grad_embed = (
        inv_rms * norm_gain * grad_normed - as_float * inv_rms * inv_rms * inv_rms * mean_term
    )
    return grad_embed.astype(jnp.bfloat16)[None]


def solution(mesh):
    in_specs = (
        P("dp", "ctx", None),
        P(),
        P("dp", None),
        P("dp", None),
        P("dp", "ctx", None),
        P("dp", "ctx", None),
        P("dp", None),
        P("dp", None),
    )
    out_specs = P("dp", "ctx", None)
    return jax.shard_map(body, mesh=mesh, in_specs=in_specs, out_specs=out_specs, check_vma=False)
```

```python
import functools

import jax
import jax.numpy as jnp
from jax import lax
from jax.experimental import pallas as pl
from jax.experimental.pallas import tpu as pltpu
from jax.sharding import PartitionSpec as P

HEADS = 32
KV_HEADS = 4
HEAD = 128
DOC_BLOCK = 128


def attn_kernel(q_ref, do_ref, k_ref, v_ref, qpos_ref, qdoc_ref, kpos_ref, kdoc_ref,
                out_ref, kg_acc, vg_acc, *, group_size, score_scale):
    allowed = (kpos_ref[...] <= qpos_ref[...]) & (kdoc_ref[...] == qdoc_ref[...])
    key_block = k_ref[...]
    value_block = v_ref[...]
    kg_acc[...] = jnp.zeros_like(kg_acc)
    vg_acc[...] = jnp.zeros_like(vg_acc)
    nt = (((1,), (1,)), ((), ()))
    tn = (((0,), (0,)), ((), ()))

    def head_step(h, carry):
        col = pl.multiple_of(h * HEAD, HEAD)
        q_h = q_ref[:, pl.ds(col, HEAD)]
        do_h = do_ref[:, pl.ds(col, HEAD)]
        raw = lax.dot_general(q_h, key_block, nt, preferred_element_type=jnp.float32)
        scores = jnp.where(allowed, raw * score_scale, -jnp.inf)
        row_max = jnp.max(scores, axis=1, keepdims=True)
        raised = jnp.exp(scores - row_max)
        soft = raised / jnp.sum(raised, axis=1, keepdims=True)
        soft_half = soft.astype(jnp.bfloat16)
        attn = jnp.dot(soft_half, value_block, preferred_element_type=jnp.float32)
        delta = jnp.sum(attn * do_h.astype(jnp.float32), axis=1, keepdims=True)
        dprobs = lax.dot_general(do_h, value_block, nt, preferred_element_type=jnp.float32)
        grad = (soft * (dprobs - delta) * score_scale).astype(jnp.bfloat16)
        kg_acc[...] += lax.dot_general(grad, q_h, tn, preferred_element_type=jnp.float32)
        vg_acc[...] += lax.dot_general(soft_half, do_h, tn, preferred_element_type=jnp.float32)
        return carry

    lax.fori_loop(0, group_size, head_step, 0)
    out_ref[:, :HEAD] = kg_acc[...].astype(out_ref.dtype)
    out_ref[:, HEAD:] = vg_acc[...].astype(out_ref.dtype)


def attend_all(queries, d_out, all_kv, qpos, qdoc, kpos, kdoc, kv_heads):
    tok_rows, width = queries.shape
    seq_len = all_kv.shape[0]
    group_size = width // (kv_heads * HEAD)
    kern = functools.partial(attn_kernel, group_size=group_size, score_scale=HEAD ** (-0.5))
    gw = group_size * HEAD
    return pl.pallas_call(
        kern,
        grid=(kv_heads,),
        in_specs=[
            pl.BlockSpec((tok_rows, gw), lambda g: (0, g)),
            pl.BlockSpec((tok_rows, gw), lambda g: (0, g)),
            pl.BlockSpec((seq_len, HEAD), lambda g: (0, 2 * g)),
            pl.BlockSpec((seq_len, HEAD), lambda g: (0, 2 * g + 1)),
            pl.BlockSpec((tok_rows, 1), lambda g: (0, 0)),
            pl.BlockSpec((tok_rows, 1), lambda g: (0, 0)),
            pl.BlockSpec((1, seq_len), lambda g: (0, 0)),
            pl.BlockSpec((1, seq_len), lambda g: (0, 0)),
        ],
        out_specs=pl.BlockSpec((seq_len, 2 * HEAD), lambda g: (0, g)),
        out_shape=jax.ShapeDtypeStruct((seq_len, 2 * kv_heads * HEAD), jnp.bfloat16),
        scratch_shapes=[pltpu.VMEM((seq_len, HEAD), jnp.float32),
                        pltpu.VMEM((seq_len, HEAD), jnp.float32)],
    )(queries, d_out, all_kv, all_kv, qpos, qdoc, kpos, kdoc)


def gather_weights(local_w, ctx_ways):
    shard_rows = local_w.shape[0]
    piece_rows = shard_rows // ctx_ways
    start = lax.axis_index("ctx") * piece_rows
    piece = lax.dynamic_slice_in_dim(local_w, start, piece_rows, axis=0)
    by_shard = lax.all_gather(piece, "dp", axis=0, tiled=False)
    full = lax.all_gather(by_shard, "ctx", axis=1, tiled=False)
    return full.reshape(-1, local_w.shape[1])


def body(embeds, norm_gain, w_key, w_value, queries, d_out, block_doc, slot_order):
    embed_rows = embeds[0]
    tok_rows = embed_rows.shape[0]
    ctx_ways = lax.axis_size("ctx")
    seq_len = tok_rows * ctx_ways
    half_len = tok_rows // 2
    as_float = embed_rows.astype(jnp.float32)
    inv_rms = lax.rsqrt(jnp.mean(as_float * as_float, axis=-1, keepdims=True) + 1e-05)
    normed = (as_float * inv_rms * norm_gain).astype(jnp.bfloat16)
    shard_rows = w_key.shape[0]
    local_w = jnp.stack(
        [w_key.reshape(shard_rows, KV_HEADS, HEAD), w_value.reshape(shard_rows, KV_HEADS, HEAD)],
        axis=2,
    ).reshape(shard_rows, 2 * KV_HEADS * HEAD)
    weights = gather_weights(local_w, ctx_ways)
    local_kv = jnp.dot(normed, weights, preferred_element_type=jnp.float32).astype(jnp.bfloat16)
    all_kv = lax.all_gather(local_kv, "ctx", axis=0, tiled=True)
    row_ids = jnp.arange(seq_len, dtype=jnp.int32)
    slot_hit = (row_ids // half_len)[:, None] == jnp.arange(2 * ctx_ways, dtype=jnp.int32)[None, :]
    key_pos = (
        jnp.sum(jnp.where(slot_hit, slot_order[0][None, :], 0), axis=1) * half_len
        + row_ids % half_len
    )
    block_hit = (key_pos // DOC_BLOCK)[:, None] == jnp.arange(block_doc.shape[1], dtype=jnp.int32)[
        None, :
    ]
    key_doc = jnp.sum(jnp.where(block_hit, block_doc[0][None, :], 0), axis=1)
    row_start = lax.axis_index("ctx") * tok_rows
    query_pos = lax.dynamic_slice_in_dim(key_pos, row_start, tok_rows)
    query_doc = lax.dynamic_slice_in_dim(key_doc, row_start, tok_rows)
    grad_terms = attend_all(
        queries[0], d_out[0], all_kv, query_pos[:, None], query_doc[:, None],
        key_pos[None, :], key_doc[None, :], KV_HEADS,
    )
    own_sum = lax.psum_scatter(grad_terms, "ctx", scatter_dimension=0, tiled=True)
    contract = (((1,), (1,)), ((), ()))
    grad_normed = lax.dot_general(own_sum, weights, contract, preferred_element_type=jnp.float32)
    mean_term = jnp.mean(as_float * norm_gain * grad_normed, axis=-1, keepdims=True)
    grad_embed = (
        inv_rms * norm_gain * grad_normed - as_float * inv_rms * inv_rms * inv_rms * mean_term
    )
    return grad_embed.astype(jnp.bfloat16)[None]


def solution(mesh):
    in_specs = (
        P("dp", "ctx", None),
        P(),
        P("dp", None),
        P("dp", None),
        P("dp", "ctx", None),
        P("dp", "ctx", None),
        P("dp", None),
        P("dp", None),
    )
    out_specs = P("dp", "ctx", None)
    return jax.shard_map(body, mesh=mesh, in_specs=in_specs, out_specs=out_specs, check_vma=False)
```

```python
import functools

import jax
import jax.numpy as jnp
from jax import lax
from jax.experimental import pallas as pl
from jax.experimental.pallas import tpu as pltpu
from jax.sharding import Mesh, PartitionSpec as P

HEADS = 32
KV_HEADS = 4
HEAD = 128
DOC_BLOCK = 128


def attn_kernel(q_ref, do_ref, k_ref, v_ref, qpos_ref, qdoc_ref, kpos_ref, kdoc_ref,
                out_ref, kg_acc, vg_acc, *, group_size, score_scale):
    allowed = (kpos_ref[...] <= qpos_ref[...]) & (kdoc_ref[...] == qdoc_ref[...])
    key_block = k_ref[...]
    value_block = v_ref[...]
    kg_acc[...] = jnp.zeros_like(kg_acc)
    vg_acc[...] = jnp.zeros_like(vg_acc)
    nt = (((1,), (1,)), ((), ()))
    tn = (((0,), (0,)), ((), ()))

    def head_step(h, carry):
        col = pl.multiple_of(h * HEAD, HEAD)
        q_h = q_ref[:, pl.ds(col, HEAD)]
        do_h = do_ref[:, pl.ds(col, HEAD)]
        raw = lax.dot_general(q_h, key_block, nt, preferred_element_type=jnp.float32)
        scores = jnp.where(allowed, raw * score_scale, -jnp.inf)
        row_max = jnp.max(scores, axis=1, keepdims=True)
        raised = jnp.exp(scores - row_max)
        soft = raised / jnp.sum(raised, axis=1, keepdims=True)
        soft_half = soft.astype(jnp.bfloat16)
        attn = jnp.dot(soft_half, value_block, preferred_element_type=jnp.float32)
        delta = jnp.sum(attn * do_h.astype(jnp.float32), axis=1, keepdims=True)
        dprobs = lax.dot_general(do_h, value_block, nt, preferred_element_type=jnp.float32)
        grad = (soft * (dprobs - delta) * score_scale).astype(jnp.bfloat16)
        kg_acc[...] += lax.dot_general(grad, q_h, tn, preferred_element_type=jnp.float32)
        vg_acc[...] += lax.dot_general(soft_half, do_h, tn, preferred_element_type=jnp.float32)
        return carry

    lax.fori_loop(0, group_size, head_step, 0)
    out_ref[:, :HEAD] = kg_acc[...].astype(out_ref.dtype)
    out_ref[:, HEAD:] = vg_acc[...].astype(out_ref.dtype)


def attend_all(queries, d_out, all_kv, qpos, qdoc, kpos, kdoc, kv_heads):
    tok_rows, width = queries.shape
    seq_len = all_kv.shape[0]
    group_size = width // (kv_heads * HEAD)
    kern = functools.partial(attn_kernel, group_size=group_size, score_scale=HEAD ** (-0.5))
    gw = group_size * HEAD
    return pl.pallas_call(
        kern,
        grid=(kv_heads,),
        in_specs=[
            pl.BlockSpec((tok_rows, gw), lambda g: (0, g)),
            pl.BlockSpec((tok_rows, gw), lambda g: (0, g)),
            pl.BlockSpec((seq_len, HEAD), lambda g: (0, 2 * g)),
            pl.BlockSpec((seq_len, HEAD), lambda g: (0, 2 * g + 1)),
            pl.BlockSpec((tok_rows, 1), lambda g: (0, 0)),
            pl.BlockSpec((tok_rows, 1), lambda g: (0, 0)),
            pl.BlockSpec((1, seq_len), lambda g: (0, 0)),
            pl.BlockSpec((1, seq_len), lambda g: (0, 0)),
        ],
        out_specs=pl.BlockSpec((seq_len, 2 * HEAD), lambda g: (0, g)),
        out_shape=jax.ShapeDtypeStruct((seq_len, 2 * kv_heads * HEAD), jnp.bfloat16),
        scratch_shapes=[pltpu.VMEM((seq_len, HEAD), jnp.float32),
                        pltpu.VMEM((seq_len, HEAD), jnp.float32)],
    )(queries, d_out, all_kv, all_kv, qpos, qdoc, kpos, kdoc)


CTX = ("chip", "core")


def gather_weights(local_w, ctx_ways):
    dp_ways = lax.axis_size("dp")
    shard_rows = local_w.shape[0]
    piece_rows = shard_rows // ctx_ways
    start = lax.axis_index(CTX) * piece_rows
    piece = lax.dynamic_slice_in_dim(local_w, start, piece_rows, axis=0)
    spread = jnp.broadcast_to(piece[None], (dp_ways,) + piece.shape)
    by_shard = lax.all_to_all(spread, "dp", 0, 0, tiled=False)
    full = lax.all_gather(by_shard, CTX, axis=1, tiled=False)
    return full.reshape(-1, local_w.shape[1])


def scatter_sum(terms, tok_rows):
    core_ways = lax.axis_size("core")
    chip_ways = lax.axis_size("chip")
    width = terms.shape[1]
    mine = lax.all_to_all(
        terms.reshape(chip_ways, core_ways, tok_rows, width), "core", 1, 1, tiled=False
    )
    mine = jnp.sum(mine.astype(jnp.float32), axis=1).astype(jnp.bfloat16)
    mine = lax.all_to_all(mine, "chip", 0, 0, tiled=False)
    return jnp.sum(mine.astype(jnp.float32), axis=0).astype(jnp.bfloat16)


def body(embeds, norm_gain, w_key, w_value, queries, d_out, block_doc, slot_order):
    embed_rows = embeds[0]
    tok_rows = embed_rows.shape[0]
    ctx_ways = lax.axis_size(CTX)
    seq_len = tok_rows * ctx_ways
    half_len = tok_rows // 2
    as_float = embed_rows.astype(jnp.float32)
    inv_rms = lax.rsqrt(jnp.mean(as_float * as_float, axis=-1, keepdims=True) + 1e-05)
    normed = (as_float * inv_rms * norm_gain).astype(jnp.bfloat16)
    shard_rows = w_key.shape[0]
    local_w = jnp.stack(
        [w_key.reshape(shard_rows, KV_HEADS, HEAD), w_value.reshape(shard_rows, KV_HEADS, HEAD)],
        axis=2,
    ).reshape(shard_rows, 2 * KV_HEADS * HEAD)
    weights = gather_weights(local_w, ctx_ways)
    local_kv = jnp.dot(normed, weights, preferred_element_type=jnp.float32).astype(jnp.bfloat16)
    all_kv = lax.all_gather(local_kv, CTX, axis=0, tiled=True)
    row_ids = jnp.arange(seq_len, dtype=jnp.int32)
    slot_hit = (row_ids // half_len)[:, None] == jnp.arange(2 * ctx_ways, dtype=jnp.int32)[None, :]
    key_pos = (
        jnp.sum(jnp.where(slot_hit, slot_order[0][None, :], 0), axis=1) * half_len
        + row_ids % half_len
    )
    block_hit = (key_pos // DOC_BLOCK)[:, None] == jnp.arange(block_doc.shape[1], dtype=jnp.int32)[
        None, :
    ]
    key_doc = jnp.sum(jnp.where(block_hit, block_doc[0][None, :], 0), axis=1)
    row_start = lax.axis_index(CTX) * tok_rows
    query_pos = lax.dynamic_slice_in_dim(key_pos, row_start, tok_rows)
    query_doc = lax.dynamic_slice_in_dim(key_doc, row_start, tok_rows)
    grad_terms = attend_all(
        queries[0], d_out[0], all_kv, query_pos[:, None], query_doc[:, None],
        key_pos[None, :], key_doc[None, :], KV_HEADS,
    )
    own_sum = scatter_sum(grad_terms, tok_rows)
    contract = (((1,), (1,)), ((), ()))
    grad_normed = lax.dot_general(own_sum, weights, contract, preferred_element_type=jnp.float32)
    mean_term = jnp.mean(as_float * norm_gain * grad_normed, axis=-1, keepdims=True)
    grad_embed = (
        inv_rms * norm_gain * grad_normed - as_float * inv_rms * inv_rms * inv_rms * mean_term
    )
    return grad_embed.astype(jnp.bfloat16)[None]


def solution(mesh):
    dp_ways, ctx_ways = mesh.shape["dp"], mesh.shape["ctx"]
    fine = Mesh(mesh.devices.reshape(dp_ways, ctx_ways // 2, 2), ("dp",) + CTX)
    in_specs = (
        P("dp", CTX, None),
        P(),
        P("dp", None),
        P("dp", None),
        P("dp", CTX, None),
        P("dp", CTX, None),
        P("dp", None),
        P("dp", None),
    )
    out_specs = P("dp", CTX, None)
    return jax.shard_map(body, mesh=fine, in_specs=in_specs, out_specs=out_specs, check_vma=False)
```

```python
import functools

import jax
import jax.numpy as jnp
from jax import lax
from jax.experimental import pallas as pl
from jax.experimental.pallas import tpu as pltpu
from jax.sharding import Mesh, PartitionSpec as P

HEADS = 32
KV_HEADS = 4
HEAD = 128
DOC_BLOCK = 128


def attn_kernel(q_ref, do_ref, k_ref, v_ref, qpos_ref, qdoc_ref, kpos_ref, kdoc_ref,
                out_ref, kg_acc, vg_acc, *, group_size, score_scale):
    allowed = (kpos_ref[...] <= qpos_ref[...]) & (kdoc_ref[...] == qdoc_ref[...])
    key_block = k_ref[...]
    value_block = v_ref[...]
    kg_acc[...] = jnp.zeros_like(kg_acc)
    vg_acc[...] = jnp.zeros_like(vg_acc)
    nt = (((1,), (1,)), ((), ()))
    tn = (((0,), (0,)), ((), ()))

    def head_step(h, carry):
        col = pl.multiple_of(h * HEAD, HEAD)
        q_h = q_ref[:, pl.ds(col, HEAD)]
        do_h = do_ref[:, pl.ds(col, HEAD)]
        raw = lax.dot_general(q_h, key_block, nt, preferred_element_type=jnp.float32)
        scores = jnp.where(allowed, raw * score_scale, -jnp.inf)
        row_max = jnp.max(scores, axis=1, keepdims=True)
        raised = jnp.exp(scores - row_max)
        soft = raised / jnp.sum(raised, axis=1, keepdims=True)
        soft_half = soft.astype(jnp.bfloat16)
        attn = jnp.dot(soft_half, value_block, preferred_element_type=jnp.float32)
        delta = jnp.sum(attn * do_h.astype(jnp.float32), axis=1, keepdims=True)
        dprobs = lax.dot_general(do_h, value_block, nt, preferred_element_type=jnp.float32)
        grad = (soft * (dprobs - delta) * score_scale).astype(jnp.bfloat16)
        kg_acc[...] += lax.dot_general(grad, q_h, tn, preferred_element_type=jnp.float32)
        vg_acc[...] += lax.dot_general(soft_half, do_h, tn, preferred_element_type=jnp.float32)
        return carry

    lax.fori_loop(0, group_size, head_step, 0)
    out_ref[:, :HEAD] = kg_acc[...].astype(out_ref.dtype)
    out_ref[:, HEAD:] = vg_acc[...].astype(out_ref.dtype)


def attend_all(queries, d_out, all_kv, qpos, qdoc, kpos, kdoc, kv_heads):
    tok_rows, width = queries.shape
    seq_len = all_kv.shape[0]
    group_size = width // (kv_heads * HEAD)
    kern = functools.partial(attn_kernel, group_size=group_size, score_scale=HEAD ** (-0.5))
    gw = group_size * HEAD
    return pl.pallas_call(
        kern,
        grid=(kv_heads,),
        in_specs=[
            pl.BlockSpec((tok_rows, gw), lambda g: (0, g)),
            pl.BlockSpec((tok_rows, gw), lambda g: (0, g)),
            pl.BlockSpec((seq_len, HEAD), lambda g: (0, 2 * g)),
            pl.BlockSpec((seq_len, HEAD), lambda g: (0, 2 * g + 1)),
            pl.BlockSpec((tok_rows, 1), lambda g: (0, 0)),
            pl.BlockSpec((tok_rows, 1), lambda g: (0, 0)),
            pl.BlockSpec((1, seq_len), lambda g: (0, 0)),
            pl.BlockSpec((1, seq_len), lambda g: (0, 0)),
        ],
        out_specs=pl.BlockSpec((seq_len, 2 * HEAD), lambda g: (0, g)),
        out_shape=jax.ShapeDtypeStruct((seq_len, 2 * kv_heads * HEAD), jnp.bfloat16),
        scratch_shapes=[pltpu.VMEM((seq_len, HEAD), jnp.float32),
                        pltpu.VMEM((seq_len, HEAD), jnp.float32)],
    )(queries, d_out, all_kv, all_kv, qpos, qdoc, kpos, kdoc)


CTX = ("chip", "core")


def gather_weights(local_w, ctx_ways):
    dp_ways = lax.axis_size("dp")
    chip_ways = lax.axis_size("chip")
    shard_rows = local_w.shape[0]
    piece_rows = shard_rows // ctx_ways
    start = (lax.axis_index("core") * chip_ways + lax.axis_index("chip")) * piece_rows
    piece = lax.dynamic_slice_in_dim(local_w, start, piece_rows, axis=0)
    spread = jnp.broadcast_to(piece[None], (dp_ways,) + piece.shape)
    by_shard = lax.all_to_all(spread, "dp", 0, 0, tiled=False)
    by_chip = lax.all_gather(by_shard, "chip", axis=1, tiled=False)
    full = lax.all_gather(by_chip, "core", axis=1, tiled=False)
    return full.reshape(-1, local_w.shape[1])


def gather_rows(local_rows):
    by_chip = lax.all_gather(local_rows, "chip", axis=0, tiled=False)
    full = lax.all_gather(by_chip, "core", axis=0, tiled=False)
    return full.reshape(-1, local_rows.shape[1])


def scatter_sum(terms, tok_rows):
    core_ways = lax.axis_size("core")
    chip_ways = lax.axis_size("chip")
    width = terms.shape[1]
    mine = lax.all_to_all(
        terms.reshape(core_ways, chip_ways, tok_rows, width), "core", 0, 0, tiled=False
    )
    mine = jnp.sum(mine.astype(jnp.float32), axis=0).astype(jnp.bfloat16)
    mine = lax.all_to_all(mine, "chip", 0, 0, tiled=False)
    return jnp.sum(mine.astype(jnp.float32), axis=0).astype(jnp.bfloat16)


def body(embeds, norm_gain, w_key, w_value, queries, d_out, block_doc, slot_order):
    embed_rows = embeds[0]
    tok_rows = embed_rows.shape[0]
    ctx_ways = lax.axis_size(CTX)
    seq_len = tok_rows * ctx_ways
    half_len = tok_rows // 2
    as_float = embed_rows.astype(jnp.float32)
    inv_rms = lax.rsqrt(jnp.mean(as_float * as_float, axis=-1, keepdims=True) + 1e-05)
    normed = (as_float * inv_rms * norm_gain).astype(jnp.bfloat16)
    shard_rows = w_key.shape[0]
    local_w = jnp.stack(
        [w_key.reshape(shard_rows, KV_HEADS, HEAD), w_value.reshape(shard_rows, KV_HEADS, HEAD)],
        axis=2,
    ).reshape(shard_rows, 2 * KV_HEADS * HEAD)
    weights = gather_weights(local_w, ctx_ways)
    local_kv = jnp.dot(normed, weights, preferred_element_type=jnp.float32).astype(jnp.bfloat16)
    all_kv = gather_rows(local_kv)
    row_ids = jnp.arange(seq_len, dtype=jnp.int32)
    slot_hit = (row_ids // half_len)[:, None] == jnp.arange(2 * ctx_ways, dtype=jnp.int32)[None, :]
    key_pos = (
        jnp.sum(jnp.where(slot_hit, slot_order[0][None, :], 0), axis=1) * half_len
        + row_ids % half_len
    )
    block_hit = (key_pos // DOC_BLOCK)[:, None] == jnp.arange(block_doc.shape[1], dtype=jnp.int32)[
        None, :
    ]
    key_doc = jnp.sum(jnp.where(block_hit, block_doc[0][None, :], 0), axis=1)
    row_start = lax.axis_index(CTX) * tok_rows
    query_pos = lax.dynamic_slice_in_dim(key_pos, row_start, tok_rows)
    query_doc = lax.dynamic_slice_in_dim(key_doc, row_start, tok_rows)
    chip_ways = lax.axis_size("chip")
    core_ways = lax.axis_size("core")

    def gathered_order(per_row):
        return per_row.reshape(chip_ways, core_ways, tok_rows).transpose(1, 0, 2).reshape(1, -1)

    grad_terms = attend_all(
        queries[0], d_out[0], all_kv, query_pos[:, None], query_doc[:, None],
        gathered_order(key_pos), gathered_order(key_doc), KV_HEADS,
    )
    own_sum = scatter_sum(grad_terms, tok_rows)
    contract = (((1,), (1,)), ((), ()))
    grad_normed = lax.dot_general(own_sum, weights, contract, preferred_element_type=jnp.float32)
    mean_term = jnp.mean(as_float * norm_gain * grad_normed, axis=-1, keepdims=True)
    grad_embed = (
        inv_rms * norm_gain * grad_normed - as_float * inv_rms * inv_rms * inv_rms * mean_term
    )
    return grad_embed.astype(jnp.bfloat16)[None]


def solution(mesh):
    dp_ways, ctx_ways = mesh.shape["dp"], mesh.shape["ctx"]
    fine = Mesh(mesh.devices.reshape(dp_ways, ctx_ways // 2, 2), ("dp",) + CTX)
    in_specs = (
        P("dp", CTX, None),
        P(),
        P("dp", None),
        P("dp", None),
        P("dp", CTX, None),
        P("dp", CTX, None),
        P("dp", None),
        P("dp", None),
    )
    out_specs = P("dp", CTX, None)
    return jax.shard_map(body, mesh=fine, in_specs=in_specs, out_specs=out_specs, check_vma=False)
```

```python
import functools

import jax
import jax.numpy as jnp
from jax import lax
from jax.experimental import pallas as pl
from jax.experimental.pallas import tpu as pltpu
from jax.sharding import Mesh, PartitionSpec as P

HEADS = 32
KV_HEADS = 4
HEAD = 128
DOC_BLOCK = 128
MOST_BLK = 8


def attn_kernel(q_ref, do_ref, k_ref, v_ref, qpos_ref, qdoc_ref, kpos_ref, kdoc_ref,
                out_ref, kg_acc, vg_acc, *, group_size, score_scale):
    allowed = (kpos_ref[...] <= qpos_ref[...]) & (kdoc_ref[...] == qdoc_ref[...])
    key_block = k_ref[...]
    value_block = v_ref[...]
    kg_acc[...] = jnp.zeros_like(kg_acc)
    vg_acc[...] = jnp.zeros_like(vg_acc)
    nt = (((1,), (1,)), ((), ()))
    tn = (((0,), (0,)), ((), ()))

    def head_step(h, carry):
        col = pl.multiple_of(h * HEAD, HEAD)
        q_h = q_ref[:, pl.ds(col, HEAD)]
        do_h = do_ref[:, pl.ds(col, HEAD)]
        raw = lax.dot_general(q_h, key_block, nt, preferred_element_type=jnp.float32)
        scores = jnp.where(allowed, raw * score_scale, -jnp.inf)
        row_max = jnp.max(scores, axis=1, keepdims=True)
        raised = jnp.exp(scores - row_max)
        soft = raised * (1.0 / jnp.sum(raised, axis=1, keepdims=True))
        soft_half = soft.astype(jnp.bfloat16)
        attn = jnp.dot(soft_half, value_block, preferred_element_type=jnp.float32)
        delta = jnp.sum(attn * do_h.astype(jnp.float32), axis=1, keepdims=True)
        dprobs = lax.dot_general(do_h, value_block, nt, preferred_element_type=jnp.float32)
        grad = (soft * (dprobs - delta) * score_scale).astype(jnp.bfloat16)
        kg_acc[...] += lax.dot_general(grad, q_h, tn, preferred_element_type=jnp.float32)
        vg_acc[...] += lax.dot_general(soft_half, do_h, tn, preferred_element_type=jnp.float32)
        return carry

    lax.fori_loop(0, group_size, head_step, 0)
    out_ref[:, :HEAD] = kg_acc[...].astype(out_ref.dtype)
    out_ref[:, HEAD:] = vg_acc[...].astype(out_ref.dtype)


def attend_all(queries, d_out, packed_kv, qpos, qdoc, kpos, kdoc, kv_heads, slot_rows):
    tok_rows, width = queries.shape
    q_slots, live_len = packed_kv.shape[0], packed_kv.shape[1]
    group_size = width // (kv_heads * HEAD)
    kern = functools.partial(attn_kernel, group_size=group_size, score_scale=HEAD ** (-0.5))
    gw = group_size * HEAD
    return pl.pallas_call(
        kern,
        grid=(kv_heads, q_slots),
        in_specs=[
            pl.BlockSpec((slot_rows, gw), lambda g, s: (s, g)),
            pl.BlockSpec((slot_rows, gw), lambda g, s: (s, g)),
            pl.BlockSpec((None, live_len, HEAD), lambda g, s: (s, 0, 2 * g)),
            pl.BlockSpec((None, live_len, HEAD), lambda g, s: (s, 0, 2 * g + 1)),
            pl.BlockSpec((slot_rows, 1), lambda g, s: (s, 0)),
            pl.BlockSpec((slot_rows, 1), lambda g, s: (s, 0)),
            pl.BlockSpec((None, 1, live_len), lambda g, s: (s, 0, 0)),
            pl.BlockSpec((None, 1, live_len), lambda g, s: (s, 0, 0)),
        ],
        out_specs=pl.BlockSpec((None, live_len, 2 * HEAD), lambda g, s: (s, 0, g)),
        out_shape=jax.ShapeDtypeStruct((q_slots, live_len, 2 * kv_heads * HEAD), jnp.float32),
        scratch_shapes=[pltpu.VMEM((live_len, HEAD), jnp.float32),
                        pltpu.VMEM((live_len, HEAD), jnp.float32)],
    )(queries, d_out, packed_kv, packed_kv, qpos, qdoc, kpos, kdoc)


CTX = ("chip", "core")


def gather_weights(local_w, ctx_ways):
    dp_ways = lax.axis_size("dp")
    shard_rows = local_w.shape[0]
    piece_rows = shard_rows // ctx_ways
    start = lax.axis_index(CTX) * piece_rows
    piece = lax.dynamic_slice_in_dim(local_w, start, piece_rows, axis=0)
    spread = jnp.broadcast_to(piece[None], (dp_ways,) + piece.shape)
    by_shard = lax.all_to_all(spread, "dp", 0, 0, tiled=False)
    full = lax.all_gather(by_shard, CTX, axis=1, tiled=False)
    return full.reshape(-1, local_w.shape[1])


def scatter_sum(terms, tok_rows):
    core_ways = lax.axis_size("core")
    chip_ways = lax.axis_size("chip")
    width = terms.shape[1]
    mine = lax.all_to_all(
        terms.reshape(chip_ways, core_ways, tok_rows, width), "core", 1, 1, tiled=False
    )
    mine = jnp.sum(mine.astype(jnp.float32), axis=1).astype(jnp.bfloat16)
    mine = lax.all_to_all(mine, "chip", 0, 0, tiled=False)
    return jnp.sum(mine.astype(jnp.float32), axis=0).astype(jnp.bfloat16)


def body(embeds, norm_gain, w_key, w_value, queries, d_out, block_doc, slot_order):
    embed_rows = embeds[0]
    tok_rows = embed_rows.shape[0]
    ctx_ways = lax.axis_size(CTX)
    seq_len = tok_rows * ctx_ways
    half_len = tok_rows // 2
    as_float = embed_rows.astype(jnp.float32)
    inv_rms = lax.rsqrt(jnp.mean(as_float * as_float, axis=-1, keepdims=True) + 1e-05)
    normed = (as_float * inv_rms * norm_gain).astype(jnp.bfloat16)
    shard_rows = w_key.shape[0]
    local_w = jnp.stack(
        [w_key.reshape(shard_rows, KV_HEADS, HEAD), w_value.reshape(shard_rows, KV_HEADS, HEAD)],
        axis=2,
    ).reshape(shard_rows, 2 * KV_HEADS * HEAD)
    weights = gather_weights(local_w, ctx_ways)
    local_kv = jnp.dot(normed, weights, preferred_element_type=jnp.float32).astype(jnp.bfloat16)
    all_kv = lax.all_gather(local_kv, CTX, axis=0, tiled=True)
    row_ids = jnp.arange(seq_len, dtype=jnp.int32)
    slot_hit = (row_ids // half_len)[:, None] == jnp.arange(2 * ctx_ways, dtype=jnp.int32)[None, :]
    key_pos = (
        jnp.sum(jnp.where(slot_hit, slot_order[0][None, :], 0), axis=1) * half_len
        + row_ids % half_len
    )
    block_hit = (key_pos // DOC_BLOCK)[:, None] == jnp.arange(block_doc.shape[1], dtype=jnp.int32)[
        None, :
    ]
    key_doc = jnp.sum(jnp.where(block_hit, block_doc[0][None, :], 0), axis=1)
    row_start = lax.axis_index(CTX) * tok_rows
    query_pos = lax.dynamic_slice_in_dim(key_pos, row_start, tok_rows)
    query_doc = lax.dynamic_slice_in_dim(key_doc, row_start, tok_rows)
    n_slots = seq_len // half_len
    q_slots = tok_rows // half_len
    live_slots = min(n_slots, MOST_BLK * DOC_BLOCK // half_len)
    slot_pos = key_pos.reshape(n_slots, half_len)[:, 0]
    slot_doc = key_doc.reshape(n_slots, half_len)[:, 0]
    own_slots = lax.axis_index(CTX) * q_slots + jnp.arange(q_slots, dtype=jnp.int32)
    live = (slot_doc[None, :] == slot_doc[own_slots][:, None]) & (
        slot_pos[None, :] <= slot_pos[own_slots][:, None]
    )
    slot_ids = jnp.arange(n_slots, dtype=jnp.int32)
    rank = jnp.where(live, 0, n_slots) + slot_ids[None, :]
    picked = jnp.argsort(rank, axis=1)[:, :live_slots]
    valid = jnp.take_along_axis(live, picked, axis=1)
    packed_kv = all_kv.reshape(n_slots, half_len, -1)[picked].reshape(q_slots, live_slots * half_len, -1)
    far = jnp.int32(seq_len)
    packed_pos = jnp.where(valid[:, :, None], key_pos.reshape(n_slots, half_len)[picked], far)
    packed_doc = key_doc.reshape(n_slots, half_len)[picked]
    packed_terms = attend_all(
        queries[0], d_out[0], packed_kv, query_pos[:, None], query_doc[:, None],
        packed_pos.reshape(q_slots, 1, -1), packed_doc.reshape(q_slots, 1, -1), KV_HEADS, half_len,
    )
    grad_terms = jnp.zeros((n_slots, half_len, packed_terms.shape[-1]), jnp.float32)
    grad_terms = grad_terms.at[picked.reshape(-1)].add(
        packed_terms.reshape(q_slots * live_slots, half_len, -1)
    )
    grad_terms = grad_terms.reshape(seq_len, -1).astype(jnp.bfloat16)
    own_sum = scatter_sum(grad_terms, tok_rows)
    contract = (((1,), (1,)), ((), ()))
    grad_normed = lax.dot_general(own_sum, weights, contract, preferred_element_type=jnp.float32)
    mean_term = jnp.mean(as_float * norm_gain * grad_normed, axis=-1, keepdims=True)
    grad_embed = (
        inv_rms * norm_gain * grad_normed - as_float * inv_rms * inv_rms * inv_rms * mean_term
    )
    return grad_embed.astype(jnp.bfloat16)[None]


def solution(mesh):
    dp_ways, ctx_ways = mesh.shape["dp"], mesh.shape["ctx"]
    fine = Mesh(mesh.devices.reshape(dp_ways, ctx_ways // 2, 2), ("dp",) + CTX)
    in_specs = (
        P("dp", CTX, None),
        P(),
        P("dp", None),
        P("dp", None),
        P("dp", CTX, None),
        P("dp", CTX, None),
        P("dp", None),
        P("dp", None),
    )
    out_specs = P("dp", CTX, None)
    return jax.shard_map(body, mesh=fine, in_specs=in_specs, out_specs=out_specs, check_vma=False)
```

```python
import functools

import jax
import jax.numpy as jnp
from jax import lax
from jax.experimental import pallas as pl
from jax.experimental.pallas import tpu as pltpu
from jax.sharding import Mesh, PartitionSpec as P

HEADS = 32
KV_HEADS = 4
HEAD = 128
DOC_BLOCK = 128


def attn_kernel(q_ref, do_ref, k_ref, v_ref, qpos_ref, qdoc_ref, kpos_ref, kdoc_ref,
                out_ref, kg_acc, vg_acc, *, group_size, score_scale):
    allowed = (kpos_ref[...] <= qpos_ref[...]) & (kdoc_ref[...] == qdoc_ref[...])
    key_block = k_ref[...]
    value_block = v_ref[...]
    kg_acc[...] = jnp.zeros_like(kg_acc)
    vg_acc[...] = jnp.zeros_like(vg_acc)
    nt = (((1,), (1,)), ((), ()))
    tn = (((0,), (0,)), ((), ()))

    def head_step(h, carry):
        col = pl.multiple_of(h * HEAD, HEAD)
        q_h = q_ref[:, pl.ds(col, HEAD)]
        do_h = do_ref[:, pl.ds(col, HEAD)]
        raw = lax.dot_general(q_h, key_block, nt, preferred_element_type=jnp.float32)
        scores = jnp.where(allowed, raw * score_scale, -jnp.inf)
        row_max = jnp.max(scores, axis=1, keepdims=True)
        raised = jnp.exp(scores - row_max)
        soft = raised / jnp.sum(raised, axis=1, keepdims=True)
        soft_half = soft.astype(jnp.bfloat16)
        attn = jnp.dot(soft_half, value_block, preferred_element_type=jnp.float32)
        delta = jnp.sum(attn * do_h.astype(jnp.float32), axis=1, keepdims=True)
        dprobs = lax.dot_general(do_h, value_block, nt, preferred_element_type=jnp.float32)
        grad = (soft * (dprobs - delta) * score_scale).astype(jnp.bfloat16)
        kg_acc[...] += lax.dot_general(grad, q_h, tn, preferred_element_type=jnp.float32)
        vg_acc[...] += lax.dot_general(soft_half, do_h, tn, preferred_element_type=jnp.float32)
        return carry

    lax.fori_loop(0, group_size, head_step, 0)
    out_ref[:, :HEAD] = kg_acc[...].astype(out_ref.dtype)
    out_ref[:, HEAD:] = vg_acc[...].astype(out_ref.dtype)


def attend_all(queries, d_out, all_kv, qpos, qdoc, kpos, kdoc, kv_heads, first_head):
    tok_rows, width = queries.shape
    seq_len = all_kv.shape[0]
    group_size = HEADS // KV_HEADS
    kern = functools.partial(attn_kernel, group_size=group_size, score_scale=HEAD ** (-0.5))
    gw = group_size * HEAD
    return pl.pallas_call(
        kern,
        grid=(kv_heads,),
        in_specs=[
            pl.BlockSpec((tok_rows, gw), lambda g: (0, g + first_head)),
            pl.BlockSpec((tok_rows, gw), lambda g: (0, g + first_head)),
            pl.BlockSpec((seq_len, HEAD), lambda g: (0, 2 * g)),
            pl.BlockSpec((seq_len, HEAD), lambda g: (0, 2 * g + 1)),
            pl.BlockSpec((tok_rows, 1), lambda g: (0, 0)),
            pl.BlockSpec((tok_rows, 1), lambda g: (0, 0)),
            pl.BlockSpec((1, seq_len), lambda g: (0, 0)),
            pl.BlockSpec((1, seq_len), lambda g: (0, 0)),
        ],
        out_specs=pl.BlockSpec((seq_len, 2 * HEAD), lambda g: (0, g)),
        out_shape=jax.ShapeDtypeStruct((seq_len, 2 * kv_heads * HEAD), jnp.bfloat16),
        scratch_shapes=[pltpu.VMEM((seq_len, HEAD), jnp.float32),
                        pltpu.VMEM((seq_len, HEAD), jnp.float32)],
    )(queries, d_out, all_kv, all_kv, qpos, qdoc, kpos, kdoc)


CTX = ("chip", "core")


def gather_weights(local_w, ctx_ways):
    dp_ways = lax.axis_size("dp")
    shard_rows = local_w.shape[0]
    piece_rows = shard_rows // ctx_ways
    start = lax.axis_index(CTX) * piece_rows
    piece = lax.dynamic_slice_in_dim(local_w, start, piece_rows, axis=0)
    spread = jnp.broadcast_to(piece[None], (dp_ways,) + piece.shape)
    by_shard = lax.all_to_all(spread, "dp", 0, 0, tiled=False)
    full = lax.all_gather(by_shard, CTX, axis=1, tiled=False)
    return full.reshape(-1, local_w.shape[1])


def scatter_sum(terms, tok_rows):
    core_ways = lax.axis_size("core")
    chip_ways = lax.axis_size("chip")
    width = terms.shape[1]
    mine = lax.all_to_all(
        terms.reshape(chip_ways, core_ways, tok_rows, width), "core", 1, 1, tiled=False
    )
    mine = jnp.sum(mine.astype(jnp.float32), axis=1).astype(jnp.bfloat16)
    mine = lax.all_to_all(mine, "chip", 0, 0, tiled=False)
    return jnp.sum(mine.astype(jnp.float32), axis=0).astype(jnp.bfloat16)


def body(embeds, norm_gain, w_key, w_value, queries, d_out, block_doc, slot_order):
    embed_rows = embeds[0]
    tok_rows = embed_rows.shape[0]
    ctx_ways = lax.axis_size(CTX)
    seq_len = tok_rows * ctx_ways
    half_len = tok_rows // 2
    as_float = embed_rows.astype(jnp.float32)
    inv_rms = lax.rsqrt(jnp.mean(as_float * as_float, axis=-1, keepdims=True) + 1e-05)
    normed = (as_float * inv_rms * norm_gain).astype(jnp.bfloat16)
    shard_rows = w_key.shape[0]
    local_w = jnp.stack(
        [w_key.reshape(shard_rows, KV_HEADS, HEAD), w_value.reshape(shard_rows, KV_HEADS, HEAD)],
        axis=2,
    ).reshape(shard_rows, 2 * KV_HEADS * HEAD)
    halves = 2
    half_w = local_w.shape[1] // halves
    weights = []
    kv_parts = []
    for part in range(halves):
        part_w = gather_weights(local_w[:, part * half_w : (part + 1) * half_w], ctx_ways)
        part_kv = jnp.dot(normed, part_w, preferred_element_type=jnp.float32).astype(jnp.bfloat16)
        weights.append(part_w)
        kv_parts.append(lax.all_gather(part_kv, CTX, axis=0, tiled=True))
    row_ids = jnp.arange(seq_len, dtype=jnp.int32)
    slot_hit = (row_ids // half_len)[:, None] == jnp.arange(2 * ctx_ways, dtype=jnp.int32)[None, :]
    key_pos = (
        jnp.sum(jnp.where(slot_hit, slot_order[0][None, :], 0), axis=1) * half_len
        + row_ids % half_len
    )
    block_hit = (key_pos // DOC_BLOCK)[:, None] == jnp.arange(block_doc.shape[1], dtype=jnp.int32)[
        None, :
    ]
    key_doc = jnp.sum(jnp.where(block_hit, block_doc[0][None, :], 0), axis=1)
    row_start = lax.axis_index(CTX) * tok_rows
    query_pos = lax.dynamic_slice_in_dim(key_pos, row_start, tok_rows)
    query_doc = lax.dynamic_slice_in_dim(key_doc, row_start, tok_rows)
    part_heads = KV_HEADS // halves
    grad_parts = [
        attend_all(
            queries[0], d_out[0], kv_parts[part], query_pos[:, None], query_doc[:, None],
            key_pos[None, :], key_doc[None, :], part_heads, part * part_heads,
        )
        for part in range(halves)
    ]
    own_sum = scatter_sum(jnp.concatenate(grad_parts, axis=1), tok_rows)
    contract = (((1,), (1,)), ((), ()))
    grad_normed = lax.dot_general(
        own_sum[:, :half_w], weights[0], contract, preferred_element_type=jnp.float32
    )
    for part in range(1, halves):
        grad_normed = grad_normed + lax.dot_general(
            own_sum[:, part * half_w : (part + 1) * half_w], weights[part], contract,
            preferred_element_type=jnp.float32,
        )
    mean_term = jnp.mean(as_float * norm_gain * grad_normed, axis=-1, keepdims=True)
    grad_embed = (
        inv_rms * norm_gain * grad_normed - as_float * inv_rms * inv_rms * inv_rms * mean_term
    )
    return grad_embed.astype(jnp.bfloat16)[None]


def solution(mesh):
    dp_ways, ctx_ways = mesh.shape["dp"], mesh.shape["ctx"]
    fine = Mesh(mesh.devices.reshape(dp_ways, ctx_ways // 2, 2), ("dp",) + CTX)
    in_specs = (
        P("dp", CTX, None),
        P(),
        P("dp", None),
        P("dp", None),
        P("dp", CTX, None),
        P("dp", CTX, None),
        P("dp", None),
        P("dp", None),
    )
    out_specs = P("dp", CTX, None)
    return jax.shard_map(body, mesh=fine, in_specs=in_specs, out_specs=out_specs, check_vma=False)
```

```python
import functools

import jax
import jax.numpy as jnp
from jax import lax
from jax.experimental import pallas as pl
from jax.experimental.pallas import tpu as pltpu
from jax.sharding import Mesh, PartitionSpec as P

HEADS = 32
KV_HEADS = 4
HEAD = 128
DOC_BLOCK = 128


def attn_kernel(q_ref, do_ref, k_ref, v_ref, qpos_ref, qdoc_ref, kpos_ref, kdoc_ref,
                out_ref, kg_acc, vg_acc, *, group_size, score_scale):
    allowed = (kpos_ref[...] <= qpos_ref[...]) & (kdoc_ref[...] == qdoc_ref[...])
    key_block = k_ref[...]
    value_block = v_ref[...]
    kg_acc[...] = jnp.zeros_like(kg_acc)
    vg_acc[...] = jnp.zeros_like(vg_acc)
    nt = (((1,), (1,)), ((), ()))
    tn = (((0,), (0,)), ((), ()))

    def head_step(h, carry):
        col = pl.multiple_of(h * HEAD, HEAD)
        q_h = q_ref[:, pl.ds(col, HEAD)]
        do_h = do_ref[:, pl.ds(col, HEAD)]
        raw = lax.dot_general(q_h, key_block, nt, preferred_element_type=jnp.float32)
        scores = jnp.where(allowed, raw * score_scale, -jnp.inf)
        row_max = jnp.max(scores, axis=1, keepdims=True)
        raised = jnp.exp(scores - row_max)
        soft = raised * (1.0 / jnp.sum(raised, axis=1, keepdims=True))
        soft_half = soft.astype(jnp.bfloat16)
        attn = jnp.dot(soft_half, value_block, preferred_element_type=jnp.float32)
        delta = jnp.sum(attn * do_h.astype(jnp.float32), axis=1, keepdims=True)
        dprobs = lax.dot_general(do_h, value_block, nt, preferred_element_type=jnp.float32)
        grad = (soft * (dprobs - delta) * score_scale).astype(jnp.bfloat16)
        kg_acc[...] += lax.dot_general(grad, q_h, tn, preferred_element_type=jnp.float32)
        vg_acc[...] += lax.dot_general(soft_half, do_h, tn, preferred_element_type=jnp.float32)
        return carry

    lax.fori_loop(0, group_size, head_step, 0)
    out_ref[:, :HEAD] = kg_acc[...].astype(out_ref.dtype)
    out_ref[:, HEAD:] = vg_acc[...].astype(out_ref.dtype)


def attend_all(queries, d_out, all_kv, qpos, qdoc, kpos, kdoc, kv_heads):
    tok_rows, width = queries.shape
    seq_len = all_kv.shape[0]
    group_size = width // (kv_heads * HEAD)
    kern = functools.partial(attn_kernel, group_size=group_size, score_scale=HEAD ** (-0.5))
    gw = group_size * HEAD
    return pl.pallas_call(
        kern,
        grid=(kv_heads,),
        in_specs=[
            pl.BlockSpec((tok_rows, gw), lambda g: (0, g)),
            pl.BlockSpec((tok_rows, gw), lambda g: (0, g)),
            pl.BlockSpec((seq_len, HEAD), lambda g: (0, 2 * g)),
            pl.BlockSpec((seq_len, HEAD), lambda g: (0, 2 * g + 1)),
            pl.BlockSpec((tok_rows, 1), lambda g: (0, 0)),
            pl.BlockSpec((tok_rows, 1), lambda g: (0, 0)),
            pl.BlockSpec((1, seq_len), lambda g: (0, 0)),
            pl.BlockSpec((1, seq_len), lambda g: (0, 0)),
        ],
        out_specs=pl.BlockSpec((seq_len, 2 * HEAD), lambda g: (0, g)),
        out_shape=jax.ShapeDtypeStruct((seq_len, 2 * kv_heads * HEAD), jnp.bfloat16),
        scratch_shapes=[pltpu.VMEM((seq_len, HEAD), jnp.float32),
                        pltpu.VMEM((seq_len, HEAD), jnp.float32)],
    )(queries, d_out, all_kv, all_kv, qpos, qdoc, kpos, kdoc)


CTX = ("chip", "core")


def gather_weights(local_w, ctx_ways):
    dp_ways = lax.axis_size("dp")
    shard_rows = local_w.shape[0]
    piece_rows = shard_rows // ctx_ways
    start = lax.axis_index(CTX) * piece_rows
    piece = lax.dynamic_slice_in_dim(local_w, start, piece_rows, axis=0)
    spread = jnp.broadcast_to(piece[None], (dp_ways,) + piece.shape)
    by_shard = lax.all_to_all(spread, "dp", 0, 0, tiled=False)
    full = lax.all_gather(by_shard, CTX, axis=1, tiled=False)
    return full.reshape(-1, local_w.shape[1])


def scatter_sum(terms, tok_rows):
    core_ways = lax.axis_size("core")
    chip_ways = lax.axis_size("chip")
    width = terms.shape[1]
    mine = lax.all_to_all(
        terms.reshape(chip_ways, core_ways, tok_rows, width), "core", 1, 1, tiled=False
    )
    mine = jnp.sum(mine.astype(jnp.float32), axis=1).astype(jnp.bfloat16)
    mine = lax.all_to_all(mine, "chip", 0, 0, tiled=False)
    return jnp.sum(mine.astype(jnp.float32), axis=0).astype(jnp.bfloat16)


def body(embeds, norm_gain, w_key, w_value, queries, d_out, block_doc, slot_order):
    embed_rows = embeds[0]
    tok_rows = embed_rows.shape[0]
    ctx_ways = lax.axis_size(CTX)
    seq_len = tok_rows * ctx_ways
    half_len = tok_rows // 2
    as_float = embed_rows.astype(jnp.float32)
    inv_rms = lax.rsqrt(jnp.mean(as_float * as_float, axis=-1, keepdims=True) + 1e-05)
    normed = (as_float * inv_rms * norm_gain).astype(jnp.bfloat16)
    shard_rows = w_key.shape[0]
    local_w = jnp.stack(
        [w_key.reshape(shard_rows, KV_HEADS, HEAD), w_value.reshape(shard_rows, KV_HEADS, HEAD)],
        axis=2,
    ).reshape(shard_rows, 2 * KV_HEADS * HEAD)
    weights = gather_weights(local_w, ctx_ways)
    local_kv = jnp.dot(normed, weights, preferred_element_type=jnp.float32).astype(jnp.bfloat16)
    all_kv = lax.all_gather(local_kv, CTX, axis=0, tiled=True)
    row_ids = jnp.arange(seq_len, dtype=jnp.int32)
    slot_hit = (row_ids // half_len)[:, None] == jnp.arange(2 * ctx_ways, dtype=jnp.int32)[None, :]
    key_pos = (
        jnp.sum(jnp.where(slot_hit, slot_order[0][None, :], 0), axis=1) * half_len
        + row_ids % half_len
    )
    block_hit = (key_pos // DOC_BLOCK)[:, None] == jnp.arange(block_doc.shape[1], dtype=jnp.int32)[
        None, :
    ]
    key_doc = jnp.sum(jnp.where(block_hit, block_doc[0][None, :], 0), axis=1)
    row_start = lax.axis_index(CTX) * tok_rows
    query_pos = lax.dynamic_slice_in_dim(key_pos, row_start, tok_rows)
    query_doc = lax.dynamic_slice_in_dim(key_doc, row_start, tok_rows)
    grad_terms = attend_all(
        queries[0], d_out[0], all_kv, query_pos[:, None], query_doc[:, None],
        key_pos[None, :], key_doc[None, :], KV_HEADS,
    )
    own_sum = scatter_sum(grad_terms, tok_rows)
    contract = (((1,), (1,)), ((), ()))
    grad_normed = lax.dot_general(own_sum, weights, contract, preferred_element_type=jnp.float32)
    mean_term = jnp.mean(as_float * norm_gain * grad_normed, axis=-1, keepdims=True)
    grad_embed = (
        inv_rms * norm_gain * grad_normed - as_float * inv_rms * inv_rms * inv_rms * mean_term
    )
    return grad_embed.astype(jnp.bfloat16)[None]


def solution(mesh):
    dp_ways, ctx_ways = mesh.shape["dp"], mesh.shape["ctx"]
    fine = Mesh(mesh.devices.reshape(dp_ways, ctx_ways // 2, 2), ("dp",) + CTX)
    in_specs = (
        P("dp", CTX, None),
        P(),
        P("dp", None),
        P("dp", None),
        P("dp", CTX, None),
        P("dp", CTX, None),
        P("dp", None),
        P("dp", None),
    )
    out_specs = P("dp", CTX, None)
    return jax.shard_map(body, mesh=fine, in_specs=in_specs, out_specs=out_specs, check_vma=False)
```

```python
import functools

import jax
import jax.numpy as jnp
from jax import lax
from jax.experimental import pallas as pl
from jax.experimental.pallas import tpu as pltpu
from jax.sharding import Mesh, PartitionSpec as P

HEADS = 32
KV_HEADS = 4
HEAD = 128
DOC_BLOCK = 128


def attn_kernel(q_ref, do_ref, k_ref, v_ref, qpos_ref, qdoc_ref, kpos_ref, kdoc_ref,
                out_ref, kg_acc, vg_acc, *, group_size, score_scale):
    allowed = (kpos_ref[...] <= qpos_ref[...]) & (kdoc_ref[...] == qdoc_ref[...])
    key_block = k_ref[...]
    value_block = v_ref[...]
    kg_acc[...] = jnp.zeros_like(kg_acc)
    vg_acc[...] = jnp.zeros_like(vg_acc)
    nt = (((1,), (1,)), ((), ()))
    tn = (((0,), (0,)), ((), ()))

    def head_step(h, carry):
        col = pl.multiple_of(h * HEAD, HEAD)
        q_h = q_ref[:, pl.ds(col, HEAD)]
        do_h = do_ref[:, pl.ds(col, HEAD)]
        raw = lax.dot_general(q_h, key_block, nt, preferred_element_type=jnp.float32)
        scores = jnp.where(allowed, raw * score_scale, -jnp.inf)
        row_max = jnp.max(scores, axis=1, keepdims=True)
        raised = jnp.exp(scores - row_max)
        soft = raised * (1.0 / jnp.sum(raised, axis=1, keepdims=True))
        soft_half = soft.astype(jnp.bfloat16)
        attn = jnp.dot(soft_half, value_block, preferred_element_type=jnp.float32)
        delta = jnp.sum(attn * do_h.astype(jnp.float32), axis=1, keepdims=True)
        dprobs = lax.dot_general(do_h, value_block, nt, preferred_element_type=jnp.float32)
        grad = (soft * (dprobs - delta) * score_scale).astype(jnp.bfloat16)
        kg_acc[...] += lax.dot_general(grad, q_h, tn, preferred_element_type=jnp.float32)
        vg_acc[...] += lax.dot_general(soft_half, do_h, tn, preferred_element_type=jnp.float32)
        return carry

    lax.fori_loop(0, group_size, head_step, 0, unroll=True)
    out_ref[:, :HEAD] = kg_acc[...].astype(out_ref.dtype)
    out_ref[:, HEAD:] = vg_acc[...].astype(out_ref.dtype)


def attend_all(queries, d_out, all_kv, qpos, qdoc, kpos, kdoc, kv_heads):
    tok_rows, width = queries.shape
    seq_len = all_kv.shape[0]
    group_size = width // (kv_heads * HEAD)
    kern = functools.partial(attn_kernel, group_size=group_size, score_scale=HEAD ** (-0.5))
    gw = group_size * HEAD
    return pl.pallas_call(
        kern,
        grid=(kv_heads,),
        in_specs=[
            pl.BlockSpec((tok_rows, gw), lambda g: (0, g)),
            pl.BlockSpec((tok_rows, gw), lambda g: (0, g)),
            pl.BlockSpec((seq_len, HEAD), lambda g: (0, 2 * g)),
            pl.BlockSpec((seq_len, HEAD), lambda g: (0, 2 * g + 1)),
            pl.BlockSpec((tok_rows, 1), lambda g: (0, 0)),
            pl.BlockSpec((tok_rows, 1), lambda g: (0, 0)),
            pl.BlockSpec((1, seq_len), lambda g: (0, 0)),
            pl.BlockSpec((1, seq_len), lambda g: (0, 0)),
        ],
        out_specs=pl.BlockSpec((seq_len, 2 * HEAD), lambda g: (0, g)),
        out_shape=jax.ShapeDtypeStruct((seq_len, 2 * kv_heads * HEAD), jnp.bfloat16),
        scratch_shapes=[pltpu.VMEM((seq_len, HEAD), jnp.float32),
                        pltpu.VMEM((seq_len, HEAD), jnp.float32)],
    )(queries, d_out, all_kv, all_kv, qpos, qdoc, kpos, kdoc)


CTX = ("chip", "core")


def gather_weights(local_w, ctx_ways):
    dp_ways = lax.axis_size("dp")
    shard_rows = local_w.shape[0]
    piece_rows = shard_rows // ctx_ways
    start = lax.axis_index(CTX) * piece_rows
    piece = lax.dynamic_slice_in_dim(local_w, start, piece_rows, axis=0)
    spread = jnp.broadcast_to(piece[None], (dp_ways,) + piece.shape)
    by_shard = lax.all_to_all(spread, "dp", 0, 0, tiled=False)
    full = lax.all_gather(by_shard, CTX, axis=1, tiled=False)
    return full.reshape(-1, local_w.shape[1])


def scatter_sum(terms, tok_rows):
    core_ways = lax.axis_size("core")
    chip_ways = lax.axis_size("chip")
    width = terms.shape[1]
    mine = lax.all_to_all(
        terms.reshape(chip_ways, core_ways, tok_rows, width), "core", 1, 1, tiled=False
    )
    mine = jnp.sum(mine.astype(jnp.float32), axis=1).astype(jnp.bfloat16)
    mine = lax.all_to_all(mine, "chip", 0, 0, tiled=False)
    return jnp.sum(mine.astype(jnp.float32), axis=0).astype(jnp.bfloat16)


def body(embeds, norm_gain, w_key, w_value, queries, d_out, block_doc, slot_order):
    embed_rows = embeds[0]
    tok_rows = embed_rows.shape[0]
    ctx_ways = lax.axis_size(CTX)
    seq_len = tok_rows * ctx_ways
    half_len = tok_rows // 2
    as_float = embed_rows.astype(jnp.float32)
    inv_rms = lax.rsqrt(jnp.mean(as_float * as_float, axis=-1, keepdims=True) + 1e-05)
    normed = (as_float * inv_rms * norm_gain).astype(jnp.bfloat16)
    shard_rows = w_key.shape[0]
    local_w = jnp.stack(
        [w_key.reshape(shard_rows, KV_HEADS, HEAD), w_value.reshape(shard_rows, KV_HEADS, HEAD)],
        axis=2,
    ).reshape(shard_rows, 2 * KV_HEADS * HEAD)
    weights = gather_weights(local_w, ctx_ways)
    local_kv = jnp.dot(normed, weights, preferred_element_type=jnp.float32).astype(jnp.bfloat16)
    all_kv = lax.all_gather(local_kv, CTX, axis=0, tiled=True)
    row_ids = jnp.arange(seq_len, dtype=jnp.int32)
    slot_hit = (row_ids // half_len)[:, None] == jnp.arange(2 * ctx_ways, dtype=jnp.int32)[None, :]
    key_pos = (
        jnp.sum(jnp.where(slot_hit, slot_order[0][None, :], 0), axis=1) * half_len
        + row_ids % half_len
    )
    block_hit = (key_pos // DOC_BLOCK)[:, None] == jnp.arange(block_doc.shape[1], dtype=jnp.int32)[
        None, :
    ]
    key_doc = jnp.sum(jnp.where(block_hit, block_doc[0][None, :], 0), axis=1)
    row_start = lax.axis_index(CTX) * tok_rows
    query_pos = lax.dynamic_slice_in_dim(key_pos, row_start, tok_rows)
    query_doc = lax.dynamic_slice_in_dim(key_doc, row_start, tok_rows)
    grad_terms = attend_all(
        queries[0], d_out[0], all_kv, query_pos[:, None], query_doc[:, None],
        key_pos[None, :], key_doc[None, :], KV_HEADS,
    )
    own_sum = scatter_sum(grad_terms, tok_rows)
    contract = (((1,), (1,)), ((), ()))
    grad_normed = lax.dot_general(own_sum, weights, contract, preferred_element_type=jnp.float32)
    mean_term = jnp.mean(as_float * norm_gain * grad_normed, axis=-1, keepdims=True)
    grad_embed = (
        inv_rms * norm_gain * grad_normed - as_float * inv_rms * inv_rms * inv_rms * mean_term
    )
    return grad_embed.astype(jnp.bfloat16)[None]


def solution(mesh):
    dp_ways, ctx_ways = mesh.shape["dp"], mesh.shape["ctx"]
    fine = Mesh(mesh.devices.reshape(dp_ways, ctx_ways // 2, 2), ("dp",) + CTX)
    in_specs = (
        P("dp", CTX, None),
        P(),
        P("dp", None),
        P("dp", None),
        P("dp", CTX, None),
        P("dp", CTX, None),
        P("dp", None),
        P("dp", None),
    )
    out_specs = P("dp", CTX, None)
    return jax.shard_map(body, mesh=fine, in_specs=in_specs, out_specs=out_specs, check_vma=False)
```

```python
import functools

import jax
import jax.numpy as jnp
from jax import lax
from jax.experimental import pallas as pl
from jax.experimental.pallas import tpu as pltpu
from jax.sharding import Mesh, PartitionSpec as P

HEADS = 32
KV_HEADS = 4
HEAD = 128
DOC_BLOCK = 128


def attn_kernel(q_ref, do_ref, k_ref, v_ref, qpos_ref, qdoc_ref, kpos_ref, kdoc_ref,
                out_ref, kg_acc, vg_acc, *, group_size, score_scale):
    allowed = (kpos_ref[...] <= qpos_ref[...]) & (kdoc_ref[...] == qdoc_ref[...])
    key_block = k_ref[...]
    value_block = v_ref[...]
    kg_acc[...] = jnp.zeros_like(kg_acc)
    vg_acc[...] = jnp.zeros_like(vg_acc)
    nt = (((1,), (1,)), ((), ()))
    tn = (((0,), (0,)), ((), ()))

    def head_step(h, carry):
        col = pl.multiple_of(h * HEAD, HEAD)
        q_h = q_ref[:, pl.ds(col, HEAD)]
        do_h = do_ref[:, pl.ds(col, HEAD)]
        raw = lax.dot_general(q_h, key_block, nt, preferred_element_type=jnp.float32)
        scores = jnp.where(allowed, raw * score_scale, -jnp.inf)
        row_max = jnp.max(scores, axis=1, keepdims=True)
        raised = jnp.exp(scores - row_max)
        soft = raised * (1.0 / jnp.sum(raised, axis=1, keepdims=True))
        soft_half = soft.astype(jnp.bfloat16)
        attn = jnp.dot(soft_half, value_block, preferred_element_type=jnp.float32)
        delta = jnp.sum(attn * do_h.astype(jnp.float32), axis=1, keepdims=True)
        dprobs = lax.dot_general(do_h, value_block, nt, preferred_element_type=jnp.float32)
        grad = (soft * (dprobs - delta) * score_scale).astype(jnp.bfloat16)
        kg_acc[...] += lax.dot_general(grad, q_h, tn, preferred_element_type=jnp.float32)
        vg_acc[...] += lax.dot_general(soft_half, do_h, tn, preferred_element_type=jnp.float32)
        return carry

    lax.fori_loop(0, group_size, head_step, 0, unroll=True)
    out_ref[:, :HEAD] = kg_acc[...].astype(out_ref.dtype)
    out_ref[:, HEAD:] = vg_acc[...].astype(out_ref.dtype)


def attend_all(queries, d_out, all_kv, qpos, qdoc, kpos, kdoc, kv_heads):
    tok_rows, width = queries.shape
    seq_len = all_kv.shape[0]
    group_size = width // (kv_heads * HEAD)
    kern = functools.partial(attn_kernel, group_size=group_size, score_scale=HEAD ** (-0.5))
    gw = group_size * HEAD
    return pl.pallas_call(
        kern,
        grid=(kv_heads,),
        in_specs=[
            pl.BlockSpec((tok_rows, gw), lambda g: (0, g)),
            pl.BlockSpec((tok_rows, gw), lambda g: (0, g)),
            pl.BlockSpec((seq_len, HEAD), lambda g: (0, 2 * g)),
            pl.BlockSpec((seq_len, HEAD), lambda g: (0, 2 * g + 1)),
            pl.BlockSpec((tok_rows, 1), lambda g: (0, 0)),
            pl.BlockSpec((tok_rows, 1), lambda g: (0, 0)),
            pl.BlockSpec((1, seq_len), lambda g: (0, 0)),
            pl.BlockSpec((1, seq_len), lambda g: (0, 0)),
        ],
        out_specs=pl.BlockSpec((seq_len, 2 * HEAD), lambda g: (0, g)),
        out_shape=jax.ShapeDtypeStruct((seq_len, 2 * kv_heads * HEAD), jnp.bfloat16),
        scratch_shapes=[pltpu.VMEM((seq_len, HEAD), jnp.float32),
                        pltpu.VMEM((seq_len, HEAD), jnp.float32)],
    )(queries, d_out, all_kv, all_kv, qpos, qdoc, kpos, kdoc)


CTX = ("chip", "core")


def gather_weights(piece, ctx_ways):
    dp_ways = lax.axis_size("dp")
    spread = jnp.broadcast_to(piece[None], (dp_ways,) + piece.shape)
    by_shard = lax.all_to_all(spread, "dp", 0, 0, tiled=False)
    full = lax.all_gather(by_shard, CTX, axis=1, tiled=False)
    return full.reshape(-1, piece.shape[1])


def scatter_sum(terms, tok_rows):
    core_ways = lax.axis_size("core")
    chip_ways = lax.axis_size("chip")
    width = terms.shape[1]
    mine = lax.all_to_all(
        terms.reshape(chip_ways, core_ways, tok_rows, width), "core", 1, 1, tiled=False
    )
    mine = jnp.sum(mine.astype(jnp.float32), axis=1).astype(jnp.bfloat16)
    mine = lax.all_to_all(mine, "chip", 0, 0, tiled=False)
    return jnp.sum(mine.astype(jnp.float32), axis=0).astype(jnp.bfloat16)


def body(embeds, norm_gain, w_key, w_value, queries, d_out, block_doc, slot_order):
    embed_rows = embeds[0]
    tok_rows = embed_rows.shape[0]
    ctx_ways = lax.axis_size(CTX)
    seq_len = tok_rows * ctx_ways
    half_len = tok_rows // 2
    as_float = embed_rows.astype(jnp.float32)
    inv_rms = lax.rsqrt(jnp.mean(as_float * as_float, axis=-1, keepdims=True) + 1e-05)
    normed = (as_float * inv_rms * norm_gain).astype(jnp.bfloat16)
    piece_rows = w_key.shape[0] // ctx_ways
    start = (lax.axis_index("chip") * lax.axis_size("core") + lax.axis_index("core")) * piece_rows
    key_piece = lax.dynamic_slice_in_dim(w_key, start, piece_rows, axis=0)
    value_piece = lax.dynamic_slice_in_dim(w_value, start, piece_rows, axis=0)
    local_w = jnp.stack(
        [key_piece.reshape(piece_rows, KV_HEADS, HEAD), value_piece.reshape(piece_rows, KV_HEADS, HEAD)],
        axis=2,
    ).reshape(piece_rows, 2 * KV_HEADS * HEAD)
    weights = gather_weights(local_w, ctx_ways)
    local_kv = jnp.dot(normed, weights, preferred_element_type=jnp.float32).astype(jnp.bfloat16)
    all_kv = lax.all_gather(local_kv, CTX, axis=0, tiled=True)
    row_ids = jnp.arange(seq_len, dtype=jnp.int32)
    slot_hit = (row_ids // half_len)[:, None] == jnp.arange(2 * ctx_ways, dtype=jnp.int32)[None, :]
    key_pos = (
        jnp.sum(jnp.where(slot_hit, slot_order[0][None, :], 0), axis=1) * half_len
        + row_ids % half_len
    )
    block_hit = (key_pos // DOC_BLOCK)[:, None] == jnp.arange(block_doc.shape[1], dtype=jnp.int32)[
        None, :
    ]
    key_doc = jnp.sum(jnp.where(block_hit, block_doc[0][None, :], 0), axis=1)
    row_start = lax.axis_index(CTX) * tok_rows
    query_pos = lax.dynamic_slice_in_dim(key_pos, row_start, tok_rows)
    query_doc = lax.dynamic_slice_in_dim(key_doc, row_start, tok_rows)
    grad_terms = attend_all(
        queries[0], d_out[0], all_kv, query_pos[:, None], query_doc[:, None],
        key_pos[None, :], key_doc[None, :], KV_HEADS,
    )
    own_sum = scatter_sum(grad_terms, tok_rows)
    contract = (((1,), (1,)), ((), ()))
    grad_normed = lax.dot_general(own_sum, weights, contract, preferred_element_type=jnp.float32)
    mean_term = jnp.mean(as_float * norm_gain * grad_normed, axis=-1, keepdims=True)
    grad_embed = (
        inv_rms * norm_gain * grad_normed - as_float * inv_rms * inv_rms * inv_rms * mean_term
    )
    return grad_embed.astype(jnp.bfloat16)[None]


def solution(mesh):
    dp_ways, ctx_ways = mesh.shape["dp"], mesh.shape["ctx"]
    fine = Mesh(mesh.devices.reshape(dp_ways, ctx_ways // 2, 2), ("dp",) + CTX)
    in_specs = (
        P("dp", CTX, None),
        P(),
        P("dp", None),
        P("dp", None),
        P("dp", CTX, None),
        P("dp", CTX, None),
        P("dp", None),
        P("dp", None),
    )
    out_specs = P("dp", CTX, None)
    return jax.shard_map(body, mesh=fine, in_specs=in_specs, out_specs=out_specs, check_vma=False)
```
